32 devices in a mesh: seq: 8 (over z, x), head: 4 (over y, core).
Axes of the slice: x: 2, y: 2, z: 4, core: 2. Of those that a mesh axis runs over, the one named last changes fastest.
Arguments:
- signal: bfloat16 [4096, 128, 64], P('seq', 'head'), may hold values from -6 to 6
- step_raw: bfloat16 [4096, 128], P('seq', 'head'), may hold values from -3 to 3
- key_proj: bfloat16 [4096, 128], P('seq'), may hold values from -0.69921875 to 0.69921875
- query_proj: bfloat16 [4096, 128], P('seq'), may hold values from -0.69921875 to 0.69921875
- decay_log: float32 [128], P('head'), may hold values from -9 to -3
- skip_gain: float32 [128], P('head'), may hold values from 0.5 to 1.5
- lengths: int32 [6], replicated, may hold values from 1 to 2048, 4096 in all
- cotangent: bfloat16 [4096, 128, 64], P('seq', 'head'), may hold values from -0.59765625 to 0.59765625
Outputs:
- output: bfloat16 [4096, 128, 64], P('seq', 'head')
- grad_signal: bfloat16 [4096, 128, 64], P('seq', 'head')
- grad_keys: bfloat16 [4096, 128], P('seq')
- grad_queries: bfloat16 [4096, 128], P('seq')
The draws below stay inside these ranges and needn't reach their ends.
Inputs may be any that keep to these rules, and one draw needn't show every extreme that they name: The 6 lengths sum to 4096; the longest is exactly 2048.
All inputs are finite; a program needn't handle non-finite values.
Results may differ from the reference program's by a relative error of at most 0.001.
Values may be sent and summed in bfloat16 or wider, within the bound.
A program may use at most 128 MiB of HBM per device.

```python
import math
import jax
import jax.numpy as jnp
import numpy as np
from jax import lax

H = 128
P_SIZE = 64
N = 128
SPAN = 256
DOCS = 6
TOKENS = 4096


def levels(key, shape, split, low, top_value):
    loudness = 1.0
    for position, shards_of in split:
        steps = jax.random.uniform(jax.random.fold_in(jax.random.fold_in(key, 6), position), (shards_of,), jnp.float32, low / len(split), top_value / len(split))
        loudness = loudness * jnp.repeat(jnp.exp(steps), shape[position] // shards_of).reshape((-1,) + (1,) * (len(shape) - 1 - position))
    return loudness


def split_up(amount, total, bound, slope):
    loads = [(1 << 20) // math.isqrt(grade ** slope) + 1 for grade in range(2, amount + 1)]
    surplus, holding = total - bound - (amount - 1), [1] * (amount - 1)
    while surplus > 0:
        movable = [i for i in range(amount - 1) if holding[i] < bound]
        whole, remaining = sum([loads[i] for i in movable]), surplus
        for i in movable:
            extra = min(bound - holding[i], max(1, remaining * loads[i] // whole), surplus)
            holding[i] = holding[i] + extra
            surplus = surplus - extra
    return np.array([bound] + holding)


def uneven(rng, number_of, total, most, slope):
    if number_of == 2:
        one = jax.random.randint(rng, (), max(1, total - most), min(most, total - 1) + 1)
        return jnp.stack([one, total - one])
    sizes = jnp.asarray(split_up(number_of, total, most, slope), jnp.int32)
    pairs = (number_of - 1) // 2
    source_of, receiver = sizes[1:1 + 2 * pairs:2], sizes[2:2 + 2 * pairs:2]
    slack = jnp.minimum(source_of - 1, most - receiver)
    moved = jax.random.randint(jax.random.fold_in(rng, 1), (pairs,), 0, 1 << 20) % (slack + 1)
    sizes = sizes.at[1:1 + 2 * pairs:2].set(source_of - moved).at[2:2 + 2 * pairs:2].set(receiver + moved)
    return sizes[jax.random.permutation(jax.random.fold_in(rng, 2), number_of)]


def centred(stream_key, dims, spread, limit, cuts=(), kind=jnp.bfloat16):
    entries = spread * jax.random.normal(stream_key, dims, jnp.float32)
    if cuts:
        entries = entries * levels(stream_key, dims, cuts, -0.22, 0.18)
    return jnp.clip(entries, -limit, limit).astype(kind)


def setup_inputs(seed: int = 0) -> dict:
    seeds = jax.random.split(jax.random.key(seed), 9)
    return {
        "signal": centred(seeds[0], (TOKENS, H, P_SIZE), 1.0, 6.0, ((0, 8), (1, 4))),
        "step_raw": centred(seeds[1], (TOKENS, H), 1.0, 3.0, ((0, 8), (1, 4))),
        "key_proj": centred(seeds[2], (TOKENS, N), 0.12, 0.69921875, ((0, 8),)),
        "query_proj": centred(seeds[3], (TOKENS, N), 0.12, 0.69921875, ((0, 8),)),
        "decay_log": jnp.clip(-9.0 + 6.0 * jax.random.uniform(seeds[4], (H,), jnp.float32) ** levels(seeds[4], (H,), ((0, 4),), -0.2, 0.2), -9.0, -3.0),
        "skip_gain": jnp.clip(0.5 + 1.0 * jax.random.uniform(seeds[5], (H,), jnp.float32) ** levels(seeds[5], (H,), ((0, 4),), -0.2, 0.2), 0.5, 1.5),
        "lengths": uneven(seeds[6], DOCS, TOKENS, TOKENS // 2, 2).astype(jnp.int32),
        "cotangent": centred(seeds[7], (TOKENS, H, P_SIZE), 0.1, 0.59765625, ((0, 8), (1, 4))),
    }


highest = lax.Precision.HIGHEST

def span_pass(drive, keys_in, queries_in, logdec, segment, prior_seg, init_state):
    length_all, heads_held, lanes_held = drive.shape
    state_width = keys_in.shape[1]
    blocks_count = length_all // SPAN
    seg_blocks = segment.reshape(blocks_count, SPAN)
    previous = jnp.concatenate([jnp.reshape(prior_seg, (1,)).astype(jnp.int32), seg_blocks[:-1, -1]]).astype(jnp.int32)
    offsets = jnp.arange(SPAN, dtype=jnp.int32)
    causal = offsets[:, None] >= offsets[None, :]

    def advance(carry_state, pieces):
        drive_block, keys_block, queries_block, decay_block, seg_block, previous_seg = pieces
        local_cum = jnp.cumsum(decay_block, axis=0)
        same_doc = ((seg_block[:, None] == seg_block[None, :]) & causal)[:, :, None]
        log_gap = jnp.where(same_doc, local_cum[:, None, :] - local_cum[None, :, :], 0.0)
        weight = jnp.where(same_doc, jnp.exp(log_gap), 0.0)
        gram_block = jnp.dot(queries_block, keys_block.T, precision=highest)
        within = jnp.einsum('tsh,shp->thp', weight * gram_block[:, :, None], drive_block, precision=highest)
        entering = jnp.where((seg_block == previous_seg)[:, None], jnp.exp(local_cum), 0.0)
        carried = jnp.einsum('tn,hpn->thp', queries_block, carry_state, precision=highest) * entering[:, :, None]
        to_end = jnp.where((seg_block == seg_block[-1])[:, None], jnp.exp(local_cum[-1][None, :] - local_cum), 0.0)
        fresh_state = jnp.einsum('sh,sn,shp->hpn', to_end, keys_block, drive_block, precision=highest)
        surviving = jnp.where(seg_block[-1] == previous_seg, jnp.exp(local_cum[-1]), 0.0)
        new_state = carry_state * surviving[:, None, None] + fresh_state
        return (new_state, within + carried)
    stacked = (drive.reshape(blocks_count, SPAN, heads_held, lanes_held), keys_in.reshape(blocks_count, SPAN, state_width), queries_in.reshape(blocks_count, SPAN, state_width), logdec.reshape(blocks_count, SPAN, heads_held), seg_blocks, previous)
    last_state, scanned = lax.scan(jax.checkpoint(advance), init_state, stacked)
    return (scanned.reshape(length_all, heads_held, lanes_held), last_state)

def reference(signal, step_raw, key_proj, query_proj, decay_log, skip_gain, lengths, cotangent):
    all_tokens, heads_all, width_p = signal.shape
    state_width = key_proj.shape[1]
    stepsize = jax.nn.softplus(step_raw.astype(jnp.float32))
    decay_rate = -jnp.exp(decay_log)
    logdec = stepsize * decay_rate[None, :]
    doc_ends = jnp.cumsum(lengths).astype(jnp.int32)
    places = jnp.arange(all_tokens, dtype=jnp.int32)
    segment = lax.optimization_barrier(jnp.sum((places[:, None] >= doc_ends[None, :]).astype(jnp.int32), axis=1)).astype(jnp.int32)
    signal_f = signal.astype(jnp.float32)
    cotan_f = cotangent.astype(jnp.float32)
    drive = stepsize[:, :, None] * signal_f
    zero_state = jnp.zeros((heads_all, width_p, state_width), jnp.float32)
    prior = jnp.full((), -1, jnp.int32)

    def forward(drive_in, keys_in, queries_in):
        return span_pass(drive_in, keys_in, queries_in, logdec, segment, prior, zero_state)[0]
    scanned, pullback = jax.vjp(forward, drive, key_proj.astype(jnp.float32), query_proj.astype(jnp.float32))
    grad_drive, grad_keys, grad_queries = pullback(cotan_f)
    output = (scanned + skip_gain[None, :, None] * signal_f).astype(jnp.bfloat16)
    grad_signal = (grad_drive * stepsize[:, :, None] + skip_gain[None, :, None] * cotan_f).astype(jnp.bfloat16)
    return (output, grad_signal, grad_keys.astype(jnp.bfloat16), grad_queries.astype(jnp.bfloat16))
```

```python
import functools

import jax
import jax.numpy as jnp
from jax import lax
from jax.experimental import pallas as pl
from jax.experimental.pallas import tpu as pltpu
from jax.sharding import PartitionSpec as P

MESH = pl.DeviceIdType.MESH
F32 = jnp.float32
BF16 = jnp.bfloat16
GROUP = 4


def mm(a, b, ca=1, cb=0):
    return lax.dot_general(a, b, (((ca,), (cb,)), ((), ())), preferred_element_type=F32)


def split(a):
    hi = a.astype(BF16)
    return hi, (a - hi.astype(F32)).astype(BF16)


def mm3(a, b, ca=1, cb=0):
    return mm(a[0], b[0], ca, cb) + mm(a[0], b[1], ca, cb) + mm(a[1], b[0], ca, cb)


def kernel(
    nseq, nhead, len_ref, sig, cot, step_ref, key_ref, query_ref, dl_ref, sk_ref,
    out_ref, gs_ref, gk_ref, gq_ref,
    bh, bl, ah, al, ys, zs, macc, gh, gl, gth, gtl, km, qm, e3, f3, pass3, ss3, sd3, sk3,
    sl, dlo, passr, r1s, r1d, zss, zds, zsr, zdr, rts, rtd, ins, ind, gg, rb, agb, gacc,
    psem, xsem, zsem, tsem, hsem, asem,
):
    heads, width, tok = sig.shape
    state = key_ref.shape[1]
    blocks = 2 * GROUP
    hb = heads // blocks
    rows = hb * width
    half = tok // 2
    me, hd = lax.axis_index("seq"), lax.axis_index("head")
    x, z = lax.rem(me, 2), me // 2
    nz = nseq // 2
    partner = me + 1 - 2 * x
    first, last = z == 0, z == nz - 1

    barrier = pltpu.get_barrier_semaphore()

    def greet(seq, head):
        pl.semaphore_signal(barrier, inc=1, device_id=(seq, head), device_id_type=MESH)

    greet(partner, hd)

    @pl.when(z > 0)
    def _():
        greet(me - 2, hd)

    @pl.when(z < nz - 1)
    def _():
        greet(me + 2, hd)

    for d in range(1, nhead):
        greet(me, lax.rem(hd + d, nhead))
    pl.semaphore_wait(barrier, nhead + jnp.where(first, 0, 1) + jnp.where(last, 0, 1))

    def hblock(b):
        return pl.ds(b * hb, hb)

    def rcopy(src, dst, sems, index, seq, head=None):
        return pltpu.make_async_remote_copy(
            src_ref=src, dst_ref=dst, send_sem=sems.at[(0,) + index], recv_sem=sems.at[(1,) + index],
            device_id=(seq, hd if head is None else head), device_id_type=MESH,
        )

    start = me * tok
    end, ends = jnp.int32(0), []
    for k in range(len_ref.shape[0]):
        end = end + len_ref[k]
        ends.append(end)

    def segment(places):
        total = jnp.zeros_like(places)
        for value in ends:
            total = total + jnp.where(places >= value, 1, 0)
        return total

    seg_last = segment(start + tok - 1)
    prior = jnp.where(start > 0, segment(start - 1), -1)
    seg_col = segment(start + lax.broadcasted_iota(jnp.int32, (tok, 1), 0))
    seg_row = segment(start + lax.broadcasted_iota(jnp.int32, (1, tok), 1))
    r_id = lax.broadcasted_iota(jnp.int32, (tok, tok), 0)
    c_id = lax.broadcasted_iota(jnp.int32, (tok, tok), 1)
    upper = jnp.where(r_id <= c_id, 1.0, 0.0).astype(BF16)

    raw = step_ref[...].astype(F32)
    size = jnp.maximum(raw, 0.0) + jnp.log1p(jnp.exp(-jnp.abs(raw)))
    logdec = size * (-jnp.exp(dl_ref[:, 0:1]))
    one = logdec.astype(BF16)
    rest = logdec - one.astype(F32)
    two, three = split(rest)
    cum = mm(three, upper) + mm(two, upper) + mm(one, upper)
    mid, final = cum[:, half - 1 : half], cum[:, tok - 1 : tok]
    e = jnp.exp(cum - mid)
    f = size * jnp.exp(mid - cum)
    lanes = (heads, state)
    passing = jnp.broadcast_to(jnp.where(seg_last == prior, jnp.exp(final), 0.0), lanes)
    to_last = jnp.broadcast_to(jnp.exp(final - mid), lanes)
    to_mid = jnp.broadcast_to(jnp.exp(mid), lanes)
    for b in range(blocks):
        part = slice(b * hb, (b + 1) * hb)
        e3[b], f3[b] = e[part], f[part]
        pass3[b], ss3[b], sd3[b] = passing[part], to_last[part], to_mid[part]
        sk3[b] = sk_ref[part, :]

    rcopy(pass3, passr, psem, (), partner).start()

    keys, queries = key_ref[...], query_ref[...]
    km[...] = jnp.where(seg_col == seg_last, keys.astype(F32), 0.0).astype(BF16)
    qm[...] = jnp.where(seg_col == prior, queries.astype(F32), 0.0).astype(BF16)

    def p1(b):
        bf = sig[hblock(b)].astype(F32) * f3[b][:, None, :]
        hi, lo = split(bf.reshape(rows, tok))
        bh[b], bl[b] = hi, lo
        kk = km[...]
        sl[b] = (mm(hi, kk) + mm(lo, kk)).reshape(hb, width, state) * ss3[b][:, None, :]
        af = cot[hblock(b)].astype(F32) * e3[b][:, None, :]
        hi, lo = split(af.reshape(rows, tok))
        ah[b], al[b] = hi, lo
        qq = qm[...]
        dlo[b] = (mm(hi, qq) + mm(lo, qq)).reshape(hb, width, state) * sd3[b][:, None, :]

    def x_copy(k):
        b = (1 - x) * GROUP + k
        return (
            rcopy(sl.at[b], r1s.at[k], xsem, (0, k), partner),
            rcopy(dlo.at[b], r1d.at[k], xsem, (1, k), partner),
        )

    @pl.loop(0, GROUP)
    def _(k):
        p1((1 - x) * GROUP + k)
        for copy in x_copy(k):
            copy.start()

    @pl.loop(0, GROUP)
    def _(k):
        p1(x * GROUP + k)

    same = seg_col == seg_row
    gram = jnp.where(same & (r_id >= c_id), mm(queries, keys, 1, 1), 0.0)
    gh[...], gl[...] = split(gram)
    gram_t = jnp.where(same & (r_id <= c_id), mm(keys, queries, 1, 1), 0.0)
    gth[...], gtl[...] = split(gram_t)
    macc[...] = jnp.zeros_like(macc)
    gacc[...] = jnp.zeros_like(gacc)

    def p2(b):
        bb = (bh[b], bl[b])
        aa = (ah[b], al[b])
        b0 = (bb[0][:, :half], bb[1][:, :half])
        a0 = (aa[0][:, :half], aa[1][:, :half])
        a1 = (aa[0][:, half:], aa[1][:, half:])
        ys[b, :, :half] = mm3(b0, (gth[:half, :half], gtl[:half, :half]))
        ys[b, :, half:] = mm3(bb, (gth[:, half:], gtl[:, half:]))
        zs[b, :, half:] = mm3(a1, (gh[half:, half:], gl[half:, half:]))
        zs[b, :, :half] = mm3(aa, (gh[:, :half], gl[:, :half]))
        macc[:half, :half] += mm3(a0, b0, 0, 0)
        macc[half:, :] += mm3(a1, bb, 0, 0)

    def z_copy(k):
        return (
            rcopy(zss.at[k], zsr.at[k], zsem, (0, k), me + 2),
            rcopy(zds.at[k], zdr.at[k], zsem, (1, k), me - 2),
        )

    def t_copy(k, mine):
        b = jnp.where(mine, x, 1 - x) * GROUP + k
        return (
            rcopy(rts.at[k], ins.at[b], tsem, (0, k), partner),
            rcopy(rtd.at[k], ind.at[b], tsem, (1, k), partner),
        )

    rcopy(pass3, passr, psem, (), partner).wait_recv()

    @pl.loop(0, GROUP)
    def _(k):
        p2(2 * k)
        b = x * GROUP + k
        for copy in x_copy(k):
            copy.wait_recv()
        left = x == 0
        own, other = pass3[b][:, None, :], passr[b][:, None, :]
        pass0, pass1 = jnp.where(left, own, other), jnp.where(left, other, own)
        s0, s1 = jnp.where(left, sl[b], r1s[k]), jnp.where(left, r1s[k], sl[b])
        d0, d1 = jnp.where(left, dlo[b], r1d[k]), jnp.where(left, r1d[k], dlo[b])
        both = pass0 * pass1
        ps, pd = pass1 * s0 + s1, d0 + pass0 * d1
        to_next, to_prev = z_copy(k)

        @pl.when(first)
        def _():
            zsr[k] = jnp.zeros_like(ps)

        @pl.when(first & (nz > 1))
        def _():
            zss[k] = ps
            to_next.start()

        @pl.when(last)
        def _():
            zdr[k] = jnp.zeros_like(pd)

        @pl.when(last & (nz > 1))
        def _():
            zds[k] = pd
            to_prev.start()

        p2(2 * k + 1)

        @pl.when(z > 0)
        def _():
            to_next.wait_recv()

        @pl.when((z > 0) & (z < nz - 1))
        def _():
            zss[k] = both * zsr[k] + ps
            to_next.start()

        @pl.when(z < nz - 1)
        def _():
            to_prev.wait_recv()

        @pl.when((z > 0) & (z < nz - 1))
        def _():
            zds[k] = both * zdr[k] + pd
            to_prev.start()

        in0 = zsr[k]
        in1 = pass0 * in0 + s0
        gin1 = zdr[k]
        gin0 = pass1 * gin1 + d1
        rts[k] = jnp.where(left, in1, in0)
        rtd[k] = jnp.where(left, gin1, gin0)
        for copy in t_copy(k, True):
            copy.start()
        ins[b] = jnp.where(left, in0, in1)
        ind[b] = jnp.where(left, gin0, gin1)

    mixed = split(jnp.where(same & (r_id >= c_id), macc[...], 0.0))
    gq_local = mm(mixed[0], keys) + mm(mixed[1], keys)
    gk_local = mm(mixed[0], queries, 0, 0) + mm(mixed[1], queries, 0, 0)

    def p3(b):
        s = split((ins[b] * sd3[b][:, None, :]).reshape(rows, state))
        d = split((ind[b] * ss3[b][:, None, :]).reshape(rows, state))
        qq, kk = qm[...], km[...]
        y = ys[b] + mm(s[0], qq, 1, 1) + mm(s[1], qq, 1, 1)
        zz = zs[b] + mm(d[0], kk, 1, 1) + mm(d[1], kk, 1, 1)
        skip = sk3[b][:, 0:1][:, :, None]
        shape = (hb, width, tok)
        out_ref[hblock(b)] = (
            y.reshape(shape) * e3[b][:, None, :] + skip * sig[hblock(b)].astype(F32)
        ).astype(BF16)
        gs_ref[hblock(b)] = (
            zz.reshape(shape) * f3[b][:, None, :] + skip * cot[hblock(b)].astype(F32)
        ).astype(BF16)
        gacc[:, :state] += mm3((bh[b], bl[b]), d, 0, 0)
        gacc[:, state:] += mm3((ah[b], al[b]), s, 0, 0)

    @pl.loop(0, GROUP)
    def _(k):
        p3(x * GROUP + k)

    @pl.loop(0, GROUP)
    def _(k):
        for copy in t_copy(k, False):
            copy.wait_recv()
        p3((1 - x) * GROUP + k)

    piece = tok // nhead
    gk = gk_local + jnp.where(seg_col == seg_last, gacc[:, :state], 0.0)
    gq = gq_local + jnp.where(seg_col == prior, gacc[:, state:], 0.0)
    for j in range(nhead):
        part = slice(j * piece, (j + 1) * piece)
        gg[j, :, :state] = gk[part]
        gg[j, :, state:] = gq[part]

    def h_copy(d):
        to = lax.rem(hd + d, nhead)
        return rcopy(gg.at[to], rb.at[d], hsem, (d,), me, to)

    def a_copy(d, sender):
        to = lax.rem(hd + d, nhead)
        return rcopy(agb.at[sender], agb.at[sender], asem, (d,), me, to)

    for d in range(1, nhead):
        h_copy(d).start()
    total = gg[hd]
    for d in range(1, nhead):
        h_copy(d).wait_recv()
        total = total + rb[d]
    agb[hd] = total.astype(BF16)
    for d in range(1, nhead):
        a_copy(d, hd).start()
    for d in range(1, nhead):
        a_copy(d, lax.rem(hd + nhead - d, nhead)).wait_recv()
    for j in range(nhead):
        part = slice(j * piece, (j + 1) * piece)
        gk_ref[part, :] = agb[j, :, :state]
        gq_ref[part, :] = agb[j, :, state:]

    for d in range(1, nhead):
        h_copy(d).wait_send()
        a_copy(d, hd).wait_send()
    rcopy(pass3, passr, psem, (), partner).wait_send()

    @pl.loop(0, GROUP)
    def _(k):
        for copy in x_copy(k) + t_copy(k, True):
            copy.wait_send()
        to_next, to_prev = z_copy(k)

        @pl.when(z < nz - 1)
        def _():
            to_next.wait_send()

        @pl.when(z > 0)
        def _():
            to_prev.wait_send()


def solution(mesh):
    nseq, nhead = mesh.shape["seq"], mesh.shape["head"]

    def on_device(signal, step_raw, key_proj, query_proj, decay_log, skip_gain, lengths, cotangent):
        tok, heads, width = signal.shape
        state = key_proj.shape[1]
        blocks = 2 * GROUP
        hb = heads // blocks
        rows = hb * width
        piece = tok // nhead
        dma = pltpu.SemaphoreType.DMA
        vmem = pltpu.VMEM
        st = (hb, width, state)
        scratch = (
            [vmem((blocks, rows, tok), BF16)] * 4
            + [vmem((blocks, rows, tok), F32)] * 2
            + [vmem((tok, tok), F32)]
            + [vmem((tok, tok), BF16)] * 4
            + [vmem((tok, state), BF16)] * 2
            + [vmem((blocks, hb, tok), F32)] * 2
            + [vmem((blocks, hb, state), F32)] * 4
            + [vmem((blocks,) + st, F32)] * 2
            + [vmem((blocks, hb, state), F32)]
            + [vmem((GROUP,) + st, F32)] * 8
            + [vmem((blocks,) + st, F32)] * 2
            + [vmem((nhead, piece, 2 * state), F32)] * 2
            + [vmem((nhead, piece, 2 * state), BF16)]
            + [vmem((tok, 2 * state), F32)]
            + [dma((2,))]
            + [dma((2, 2, GROUP))] * 3
            + [dma((2, nhead))] * 2
        )
        turned = jax.ShapeDtypeStruct((heads, width, tok), BF16)
        grads = jax.ShapeDtypeStruct((tok, state), BF16)
        whole = pl.BlockSpec(memory_space=pltpu.VMEM)
        out, gs, gk, gq = pl.pallas_call(
            functools.partial(kernel, nseq, nhead),
            out_shape=(turned, turned, grads, grads),
            in_specs=[pl.BlockSpec(memory_space=pltpu.SMEM)] + [whole] * 7,
            out_specs=(whole,) * 4,
            scratch_shapes=scratch,
            compiler_params=pltpu.CompilerParams(
                collective_id=0, has_side_effects=True, vmem_limit_bytes=60 << 20
            ),
        )(
            lengths,
            jnp.transpose(signal, (1, 2, 0)),
            jnp.transpose(cotangent, (1, 2, 0)),
            step_raw.T,
            key_proj,
            query_proj,
            jnp.broadcast_to(decay_log[:, None], (heads, state)),
            jnp.broadcast_to(skip_gain[:, None], (heads, state)),
        )
        return jnp.transpose(out, (2, 0, 1)), jnp.transpose(gs, (2, 0, 1)), gk, gq

    in_specs = (
        P("seq", "head", None),
        P("seq", "head"),
        P("seq", None),
        P("seq", None),
        P("head"),
        P("head"),
        P(),
        P("seq", "head", None),
    )
    out_specs = (P("seq", "head", None), P("seq", "head", None), P("seq", None), P("seq", None))
    return jax.shard_map(
        on_device, mesh=mesh, in_specs=in_specs, out_specs=out_specs, check_vma=False
    )
```

```python
import functools

import jax
import jax.numpy as jnp
from jax import lax
from jax.experimental import pallas as pl
from jax.experimental.pallas import tpu as pltpu
from jax.sharding import PartitionSpec as P

MESH = pl.DeviceIdType.MESH
F32 = jnp.float32
BF16 = jnp.bfloat16
GROUP = 4


def mm(a, b, ca=1, cb=0):
    return lax.dot_general(a, b, (((ca,), (cb,)), ((), ())), preferred_element_type=F32)


def split(a):
    hi = a.astype(BF16)
    return hi, (a - hi.astype(F32)).astype(BF16)


def mm3(a, b, ca=1, cb=0):
    return mm(a[0], b[0], ca, cb) + mm(a[0], b[1], ca, cb) + mm(a[1], b[0], ca, cb)


def quant(v, axis):
    top = jnp.maximum(jnp.max(jnp.abs(v), axis=axis, keepdims=True), 1e-30)
    code = jnp.round(v * (32000.0 / top)).astype(jnp.int32).astype(jnp.int16)
    return code, top * (1.0 / 32000.0)


def wide(code, scale):
    return code.astype(jnp.int32).astype(F32) * scale


def kernel(
    nseq, nhead, len_ref, sig, cot, step_ref, key_ref, query_ref, dl_ref, sk_ref,
    out_ref, gs_ref, gk_ref, gq_ref,
    bh, bl, ah, al, ys, zs, macc, gh, gl, gth, gtl, km, qm, e3, f3, pass3, ss3, sd3, sk3,
    sl, dlo, zsr, zdr, ins, ind, xq, xqr, tq, tqr, xs, xsr, zq, zqr, zc, zcr, ts, tsr,
    gg, hq, hqr, hs, hsr, agb, gacc, xsem, zsem, tsem, hsem, asem,
):
    heads, width, tok = sig.shape
    state = key_ref.shape[1]
    blocks = 2 * GROUP
    hb = heads // blocks
    rows = hb * width
    half = tok // 2
    me, hd = lax.axis_index("seq"), lax.axis_index("head")
    x, z = lax.rem(me, 2), me // 2
    nz = nseq // 2
    partner = me + 1 - 2 * x
    first, last = z == 0, z == nz - 1

    barrier = pltpu.get_barrier_semaphore()

    def greet(seq, head):
        pl.semaphore_signal(barrier, inc=1, device_id=(seq, head), device_id_type=MESH)

    greet(partner, hd)

    @pl.when(z > 0)
    def _():
        greet(me - 2, hd)

    @pl.when(z < nz - 1)
    def _():
        greet(me + 2, hd)

    for d in range(1, nhead):
        greet(me, lax.rem(hd + d, nhead))
    pl.semaphore_wait(barrier, nhead + jnp.where(first, 0, 1) + jnp.where(last, 0, 1))

    def hblock(b):
        return pl.ds(b * hb, hb)

    def rcopy(src, dst, sems, index, seq, head=None):
        return pltpu.make_async_remote_copy(
            src_ref=src, dst_ref=dst, send_sem=sems.at[(0,) + index], recv_sem=sems.at[(1,) + index],
            device_id=(seq, hd if head is None else head), device_id_type=MESH,
        )

    start = me * tok
    end, ends = jnp.int32(0), []
    for k in range(len_ref.shape[0]):
        end = end + len_ref[k]
        ends.append(end)

    def segment(places):
        total = jnp.zeros_like(places)
        for value in ends:
            total = total + jnp.where(places >= value, 1, 0)
        return total

    seg_last = segment(start + tok - 1)
    prior = jnp.where(start > 0, segment(start - 1), -1)
    seg_col = segment(start + lax.broadcasted_iota(jnp.int32, (tok, 1), 0))
    seg_row = segment(start + lax.broadcasted_iota(jnp.int32, (1, tok), 1))
    r_id = lax.broadcasted_iota(jnp.int32, (tok, tok), 0)
    c_id = lax.broadcasted_iota(jnp.int32, (tok, tok), 1)
    upper = jnp.where(r_id <= c_id, 1.0, 0.0).astype(BF16)

    raw = step_ref[...].astype(F32)
    size = jnp.maximum(raw, 0.0) + jnp.log1p(jnp.exp(-jnp.abs(raw)))
    eye = lax.broadcasted_iota(jnp.int32, (heads, heads), 0) == lax.broadcasted_iota(
        jnp.int32, (heads, heads), 1
    )
    column = lambda ref: jnp.sum(jnp.where(eye, ref[...], 0.0), axis=1, keepdims=True)
    logdec = size * (-jnp.exp(column(dl_ref)))
    one = logdec.astype(BF16)
    rest = logdec - one.astype(F32)
    two, three = split(rest)
    cum = mm(three, upper) + mm(two, upper) + mm(one, upper)
    mid, final = cum[:, half - 1 : half], cum[:, tok - 1 : tok]
    e = jnp.exp(cum - mid)
    f = size * jnp.exp(mid - cum)
    lanes = (heads, state)
    passing = jnp.broadcast_to(jnp.where(seg_last == prior, jnp.exp(final), 0.0), lanes)
    to_last = jnp.broadcast_to(jnp.exp(final - mid), lanes)
    to_mid = jnp.broadcast_to(jnp.exp(mid), lanes)
    skips = jnp.broadcast_to(column(sk_ref), lanes)
    for b in range(blocks):
        part = slice(b * hb, (b + 1) * hb)
        e3[b], f3[b] = e[part], f[part]
        pass3[b], ss3[b], sd3[b] = passing[part], to_last[part], to_mid[part]
        sk3[b] = skips[part]

    keys, queries = key_ref[...], query_ref[...]
    km[...] = jnp.where(seg_col == seg_last, keys.astype(F32), 0.0).astype(BF16)
    qm[...] = jnp.where(seg_col == prior, queries.astype(F32), 0.0).astype(BF16)

    def p1(b):
        bf = sig[hblock(b)].astype(F32) * f3[b][:, None, :]
        hi, lo = split(bf.reshape(rows, tok))
        bh[b], bl[b] = hi, lo
        kk = km[...]
        sl[b] = (mm(hi, kk) + mm(lo, kk)).reshape(hb, width, state) * ss3[b][:, None, :]
        af = cot[hblock(b)].astype(F32) * e3[b][:, None, :]
        hi, lo = split(af.reshape(rows, tok))
        ah[b], al[b] = hi, lo
        qq = qm[...]
        dlo[b] = (mm(hi, qq) + mm(lo, qq)).reshape(hb, width, state) * sd3[b][:, None, :]

    def x_copy(k):
        return (
            rcopy(xq.at[k], xqr.at[k], xsem, (0, k), partner),
            rcopy(xs.at[k], xsr.at[k], xsem, (1, k), partner),
        )

    @pl.loop(0, GROUP)
    def _(k):
        b = (1 - x) * GROUP + k
        p1(b)
        code, scale = quant(sl[b], 1)
        xq[k, 0], xs[k, 0] = code, scale[:, 0, :]
        code, scale = quant(dlo[b], 1)
        xq[k, 1], xs[k, 1] = code, scale[:, 0, :]
        xs[k, 2] = pass3[b]
        for copy in x_copy(k):
            copy.start()

    @pl.loop(0, GROUP)
    def _(k):
        p1(x * GROUP + k)

    same = seg_col == seg_row
    gram = jnp.where(same & (r_id >= c_id), mm(queries, keys, 1, 1), 0.0)
    gh[...], gl[...] = split(gram)
    gram_t = jnp.where(same & (r_id <= c_id), mm(keys, queries, 1, 1), 0.0)
    gth[...], gtl[...] = split(gram_t)
    macc[...] = jnp.zeros_like(macc)
    gacc[...] = jnp.zeros_like(gacc)

    def p2(b):
        bb = (bh[b], bl[b])
        aa = (ah[b], al[b])
        b0 = (bb[0][:, :half], bb[1][:, :half])
        a0 = (aa[0][:, :half], aa[1][:, :half])
        a1 = (aa[0][:, half:], aa[1][:, half:])
        ys[b, :, :half] = mm3(b0, (gth[:half, :half], gtl[:half, :half]))
        ys[b, :, half:] = mm3(bb, (gth[:, half:], gtl[:, half:]))
        zs[b, :, half:] = mm3(a1, (gh[half:, half:], gl[half:, half:]))
        zs[b, :, :half] = mm3(aa, (gh[:, :half], gl[:, :half]))
        macc[:half, :half] += mm3(a0, b0, 0, 0)
        macc[half:, :] += mm3(a1, bb, 0, 0)

    def z_copy(k):
        return (
            (
                rcopy(zq.at[0, k], zqr.at[0, k], zsem, (0, 0, k), me + 2),
                rcopy(zc.at[0, k], zcr.at[0, k], zsem, (0, 1, k), me + 2),
            ),
            (
                rcopy(zq.at[1, k], zqr.at[1, k], zsem, (1, 0, k), me - 2),
                rcopy(zc.at[1, k], zcr.at[1, k], zsem, (1, 1, k), me - 2),
            ),
        )

    def t_copy(k):
        return (
            rcopy(tq.at[k], tqr.at[k], tsem, (0, k), partner),
            rcopy(ts.at[k], tsr.at[k], tsem, (1, k), partner),
        )

    def z_send(way, k, value, copies):
        code, scale = quant(value, 1)
        zq[way, k], zc[way, k] = code, scale[:, 0, :]
        for copy in copies:
            copy.start()

    def z_take(way, k, into, copies):
        for copy in copies:
            copy.wait_recv()
        into[k] = wide(zqr[way, k], zcr[way, k][:, None, :])

    @pl.loop(0, GROUP)
    def _(k):
        p2(2 * k)
        b = x * GROUP + k
        for copy in x_copy(k):
            copy.wait_recv()
        left = x == 0
        own, other = pass3[b][:, None, :], xsr[k, 2][:, None, :]
        s_in = wide(xqr[k, 0], xsr[k, 0][:, None, :])
        d_in = wide(xqr[k, 1], xsr[k, 1][:, None, :])
        pass0, pass1 = jnp.where(left, own, other), jnp.where(left, other, own)
        s0, s1 = jnp.where(left, sl[b], s_in), jnp.where(left, s_in, sl[b])
        d0, d1 = jnp.where(left, dlo[b], d_in), jnp.where(left, d_in, dlo[b])
        both = pass0 * pass1
        ps, pd = pass1 * s0 + s1, d0 + pass0 * d1
        to_next, to_prev = z_copy(k)

        @pl.when(first)
        def _():
            zsr[k] = jnp.zeros_like(ps)

        @pl.when(first & (nz > 1))
        def _():
            z_send(0, k, ps, to_next)

        @pl.when(last)
        def _():
            zdr[k] = jnp.zeros_like(pd)

        @pl.when(last & (nz > 1))
        def _():
            z_send(1, k, pd, to_prev)

        p2(2 * k + 1)

        @pl.when(z > 0)
        def _():
            z_take(0, k, zsr, to_next)

        @pl.when((z > 0) & (z < nz - 1))
        def _():
            z_send(0, k, both * zsr[k] + ps, to_next)

        @pl.when(z < nz - 1)
        def _():
            z_take(1, k, zdr, to_prev)

        @pl.when((z > 0) & (z < nz - 1))
        def _():
            z_send(1, k, both * zdr[k] + pd, to_prev)

        in0 = zsr[k]
        in1 = pass0 * in0 + s0
        gin1 = zdr[k]
        gin0 = pass1 * gin1 + d1
        code, scale = quant(jnp.where(left, in1, in0), 1)
        tq[k, 0], ts[k, 0] = code, scale[:, 0, :]
        code, scale = quant(jnp.where(left, gin1, gin0), 1)
        tq[k, 1], ts[k, 1] = code, scale[:, 0, :]
        for copy in t_copy(k):
            copy.start()
        ins[b] = jnp.where(left, in0, in1)
        ind[b] = jnp.where(left, gin0, gin1)

    mixed = split(jnp.where(same & (r_id >= c_id), macc[...], 0.0))
    gq_local = mm(mixed[0], keys) + mm(mixed[1], keys)
    gk_local = mm(mixed[0], queries, 0, 0) + mm(mixed[1], queries, 0, 0)

    def p3(b):
        s = split((ins[b] * sd3[b][:, None, :]).reshape(rows, state))
        d = split((ind[b] * ss3[b][:, None, :]).reshape(rows, state))
        qq, kk = qm[...], km[...]
        y = ys[b] + mm(s[0], qq, 1, 1) + mm(s[1], qq, 1, 1)
        zz = zs[b] + mm(d[0], kk, 1, 1) + mm(d[1], kk, 1, 1)
        skip = sk3[b][:, 0:1][:, :, None]
        shape = (hb, width, tok)
        out_ref[hblock(b)] = (
            y.reshape(shape) * e3[b][:, None, :] + skip * sig[hblock(b)].astype(F32)
        ).astype(BF16)
        gs_ref[hblock(b)] = (
            zz.reshape(shape) * f3[b][:, None, :] + skip * cot[hblock(b)].astype(F32)
        ).astype(BF16)
        gacc[:, :state] += mm3((bh[b], bl[b]), d, 0, 0)
        gacc[:, state:] += mm3((ah[b], al[b]), s, 0, 0)

    @pl.loop(0, GROUP)
    def _(k):
        p3(x * GROUP + k)

    @pl.loop(0, GROUP)
    def _(k):
        for copy in t_copy(k):
            copy.wait_recv()
        b = (1 - x) * GROUP + k
        ins[b] = wide(tqr[k, 0], tsr[k, 0][:, None, :])
        ind[b] = wide(tqr[k, 1], tsr[k, 1][:, None, :])
        p3(b)

    piece = tok // nhead
    gk = gk_local + jnp.where(seg_col == seg_last, gacc[:, :state], 0.0)
    gq = gq_local + jnp.where(seg_col == prior, gacc[:, state:], 0.0)
    for j in range(nhead):
        part = slice(j * piece, (j + 1) * piece)
        gg[j, :, :state] = gk[part]
        gg[j, :, state:] = gq[part]

    def h_copy(d):
        to = lax.rem(hd + d, nhead)
        return (
            rcopy(hq.at[to], hqr.at[d], hsem, (0, d), me, to),
            rcopy(hs.at[to], hsr.at[d], hsem, (1, d), me, to),
        )

    def a_copy(d, sender):
        to = lax.rem(hd + d, nhead)
        return rcopy(agb.at[sender], agb.at[sender], asem, (d,), me, to)

    for d in range(1, nhead):
        to = lax.rem(hd + d, nhead)
        code, scale = quant(gg[to], 0)
        hq[to], hs[to] = code, jnp.broadcast_to(scale, hs.shape[1:])
        for copy in h_copy(d):
            copy.start()
    total = gg[hd]
    for d in range(1, nhead):
        for copy in h_copy(d):
            copy.wait_recv()
        total = total + wide(hqr[d], hsr[d][0:1, :])
    agb[hd] = total.astype(BF16)
    for d in range(1, nhead):
        a_copy(d, hd).start()
    for d in range(1, nhead):
        a_copy(d, lax.rem(hd + nhead - d, nhead)).wait_recv()
    for j in range(nhead):
        part = slice(j * piece, (j + 1) * piece)
        gk_ref[part, :] = agb[j, :, :state]
        gq_ref[part, :] = agb[j, :, state:]

    for d in range(1, nhead):
        for copy in h_copy(d):
            copy.wait_send()
        a_copy(d, hd).wait_send()

    @pl.loop(0, GROUP)
    def _(k):
        for copy in x_copy(k) + t_copy(k):
            copy.wait_send()
        to_next, to_prev = z_copy(k)

        @pl.when(z < nz - 1)
        def _():
            for copy in to_next:
                copy.wait_send()

        @pl.when(z > 0)
        def _():
            for copy in to_prev:
                copy.wait_send()


def solution(mesh):
    nseq, nhead = mesh.shape["seq"], mesh.shape["head"]

    def on_device(signal, step_raw, key_proj, query_proj, decay_log, skip_gain, lengths, cotangent):
        tok, heads, width = signal.shape
        state = key_proj.shape[1]
        blocks = 2 * GROUP
        hb = heads // blocks
        rows = hb * width
        piece = tok // nhead
        dma = pltpu.SemaphoreType.DMA
        vmem = pltpu.VMEM
        st = (hb, width, state)
        scratch = (
            [vmem((blocks, rows, tok), BF16)] * 4
            + [vmem((blocks, rows, tok), F32)] * 2
            + [vmem((tok, tok), F32)]
            + [vmem((tok, tok), BF16)] * 4
            + [vmem((tok, state), BF16)] * 2
            + [vmem((blocks, hb, tok), F32)] * 2
            + [vmem((blocks, hb, state), F32)] * 4
            + [vmem((blocks,) + st, F32)] * 2
            + [vmem((GROUP,) + st, F32)] * 2
            + [vmem((blocks,) + st, F32)] * 2
            + [vmem((GROUP, 2) + st, jnp.int16)] * 4
            + [vmem((GROUP, 3, hb, state), F32)] * 2
            + [vmem((2, GROUP) + st, jnp.int16)] * 2
            + [vmem((2, GROUP, hb, state), F32)] * 2
            + [vmem((GROUP, 2, hb, state), F32)] * 2
            + [vmem((nhead, piece, 2 * state), F32)]
            + [vmem((nhead, piece, 2 * state), jnp.int16)] * 2
            + [vmem((nhead, 8, 2 * state), F32)] * 2
            + [vmem((nhead, piece, 2 * state), BF16)]
            + [vmem((tok, 2 * state), F32)]
            + [dma((2, 2, GROUP)), dma((2, 2, 2, GROUP)), dma((2, 2, GROUP))]
            + [dma((2, 2, nhead)), dma((2, nhead))]
        )
        turned = jax.ShapeDtypeStruct((heads, width, tok), BF16)
        grads = jax.ShapeDtypeStruct((tok, state), BF16)
        whole = pl.BlockSpec(memory_space=pltpu.VMEM)
        out, gs, gk, gq = pl.pallas_call(
            functools.partial(kernel, nseq, nhead),
            out_shape=(turned, turned, grads, grads),
            in_specs=[pl.BlockSpec(memory_space=pltpu.SMEM)] + [whole] * 7,
            out_specs=(whole,) * 4,
            scratch_shapes=scratch,
            compiler_params=pltpu.CompilerParams(
                collective_id=0, has_side_effects=True, vmem_limit_bytes=60 << 20
            ),
        )(
            lengths,
            jnp.transpose(signal, (1, 2, 0)),
            jnp.transpose(cotangent, (1, 2, 0)),
            step_raw.T,
            key_proj,
            query_proj,
            decay_log[None, :],
            skip_gain[None, :],
        )
        return jnp.transpose(out, (2, 0, 1)), jnp.transpose(gs, (2, 0, 1)), gk, gq

    in_specs = (
        P("seq", "head", None),
        P("seq", "head"),
        P("seq", None),
        P("seq", None),
        P("head"),
        P("head"),
        P(),
        P("seq", "head", None),
    )
    out_specs = (P("seq", "head", None), P("seq", "head", None), P("seq", None), P("seq", None))
    return jax.shard_map(
        on_device, mesh=mesh, in_specs=in_specs, out_specs=out_specs, check_vma=False
    )
```

```python
import functools

import jax
import jax.numpy as jnp
from jax import lax
from jax.experimental import pallas as pl
from jax.experimental.pallas import tpu as pltpu
from jax.sharding import PartitionSpec as P

MESH = pl.DeviceIdType.MESH
F32 = jnp.float32
BF16 = jnp.bfloat16
GROUP = 4


def mm(a, b, ca=1, cb=0):
    return lax.dot_general(a, b, (((ca,), (cb,)), ((), ())), preferred_element_type=F32)


def split(a):
    hi = a.astype(BF16)
    return hi, (a - hi.astype(F32)).astype(BF16)


def mm3(a, b, ca=1, cb=0):
    return mm(a[0], b[0], ca, cb) + mm(a[0], b[1], ca, cb) + mm(a[1], b[0], ca, cb)


def quant(v, axis):
    top = jnp.maximum(jnp.max(jnp.abs(v), axis=axis, keepdims=True), 1e-30)
    code = jnp.round(v * (32000.0 / top)).astype(jnp.int32).astype(jnp.int16)
    return code, top * (1.0 / 32000.0)


def wide(code, scale):
    return code.astype(jnp.int32).astype(F32) * scale


def kernel(
    nseq, nhead, len_ref, sig, cot, step_ref, key_ref, query_ref, dl_ref, sk_ref,
    out_ref, gs_ref, gk_ref, gq_ref,
    bh, bl, ah, al, ys, zs, macc, gh, gl, gth, gtl, km, qm, e3, f3, pass3, ss3, sd3, sk3,
    sl, dlo, zsr, zdr, ins, ind, xq, xqr, tq, tqr, xs, xsr, zq, zqr, zc, zcr, ts, tsr,
    gg, hq, hqr, hs, hsr, agb, gacc, xsem, zsem, tsem, hsem, asem,
):
    heads, width, tok = sig.shape
    state = key_ref.shape[1]
    blocks = 2 * GROUP
    hb = heads // blocks
    rows = hb * width
    half = tok // 2
    me, hd = lax.axis_index("seq"), lax.axis_index("head")
    x, z = lax.rem(me, 2), me // 2
    nz = nseq // 2
    partner = me + 1 - 2 * x
    first, last = z == 0, z == nz - 1

    barrier = pltpu.get_barrier_semaphore()

    def greet(seq, head):
        pl.semaphore_signal(barrier, inc=1, device_id=(seq, head), device_id_type=MESH)

    greet(partner, hd)

    @pl.when(z > 0)
    def _():
        greet(me - 2, hd)

    @pl.when(z < nz - 1)
    def _():
        greet(me + 2, hd)

    for d in range(1, nhead):
        greet(me, lax.rem(hd + d, nhead))
    pl.semaphore_wait(barrier, nhead + jnp.where(first, 0, 1) + jnp.where(last, 0, 1))

    def hblock(b):
        return pl.ds(b * hb, hb)

    def rcopy(src, dst, sems, index, seq, head=None):
        return pltpu.make_async_remote_copy(
            src_ref=src, dst_ref=dst, send_sem=sems.at[(0,) + index], recv_sem=sems.at[(1,) + index],
            device_id=(seq, hd if head is None else head), device_id_type=MESH,
        )

    start = me * tok
    end, ends = jnp.int32(0), []
    for k in range(len_ref.shape[0]):
        end = end + len_ref[k]
        ends.append(end)

    def segment(places):
        total = jnp.zeros_like(places)
        for value in ends:
            total = total + jnp.where(places >= value, 1, 0)
        return total

    seg_last = segment(start + tok - 1)
    prior = jnp.where(start > 0, segment(start - 1), -1)
    seg_col = segment(start + lax.broadcasted_iota(jnp.int32, (tok, 1), 0))
    seg_row = segment(start + lax.broadcasted_iota(jnp.int32, (1, tok), 1))
    r_id = lax.broadcasted_iota(jnp.int32, (tok, tok), 0)
    c_id = lax.broadcasted_iota(jnp.int32, (tok, tok), 1)
    upper = jnp.where(r_id <= c_id, 1.0, 0.0).astype(BF16)

    raw = step_ref[...].astype(F32)
    size = jnp.maximum(raw, 0.0) + jnp.log1p(jnp.exp(-jnp.abs(raw)))
    eye = lax.broadcasted_iota(jnp.int32, (heads, heads), 0) == lax.broadcasted_iota(
        jnp.int32, (heads, heads), 1
    )
    column = lambda ref: jnp.sum(jnp.where(eye, ref[...], 0.0), axis=1, keepdims=True)
    logdec = size * (-jnp.exp(column(dl_ref)))
    one = logdec.astype(BF16)
    rest = logdec - one.astype(F32)
    two, three = split(rest)
    cum = mm(three, upper) + mm(two, upper) + mm(one, upper)
    mid, final = cum[:, half - 1 : half], cum[:, tok - 1 : tok]
    e = jnp.exp(cum - mid)
    f = size * jnp.exp(mid - cum)
    lanes = (heads, state)
    passing = jnp.broadcast_to(jnp.where(seg_last == prior, jnp.exp(final), 0.0), lanes)
    to_last = jnp.broadcast_to(jnp.exp(final - mid), lanes)
    to_mid = jnp.broadcast_to(jnp.exp(mid), lanes)
    skips = jnp.broadcast_to(column(sk_ref), lanes)
    for b in range(blocks):
        part = slice(b * hb, (b + 1) * hb)
        e3[b], f3[b] = e[part], f[part]
        pass3[b], ss3[b], sd3[b] = passing[part], to_last[part], to_mid[part]
        sk3[b] = skips[part]

    keys, queries = key_ref[...], query_ref[...]
    km[...] = jnp.where(seg_col == seg_last, keys.astype(F32), 0.0).astype(BF16)
    qm[...] = jnp.where(seg_col == prior, queries.astype(F32), 0.0).astype(BF16)

    def p1(b):
        bf = sig[hblock(b)].astype(F32) * f3[b][:, None, :]
        hi, lo = split(bf.reshape(rows, tok))
        bh[b], bl[b] = hi, lo
        kk = km[...]
        sl[b] = (mm(hi, kk) + mm(lo, kk)).reshape(hb, width, state) * ss3[b][:, None, :]
        af = cot[hblock(b)].astype(F32) * e3[b][:, None, :]
        hi, lo = split(af.reshape(rows, tok))
        ah[b], al[b] = hi, lo
        qq = qm[...]
        dlo[b] = (mm(hi, qq) + mm(lo, qq)).reshape(hb, width, state) * sd3[b][:, None, :]

    def x_copy(k):
        return (
            rcopy(xq.at[k], xqr.at[k], xsem, (0, k), partner),
            rcopy(xs.at[k], xsr.at[k], xsem, (1, k), partner),
        )

    @pl.loop(0, GROUP)
    def _(k):
        b = (1 - x) * GROUP + k
        p1(b)
        code, scale = quant(sl[b], 1)
        xq[k, 0], xs[k, 0] = code, scale[:, 0, :]
        code, scale = quant(dlo[b], 1)
        xq[k, 1], xs[k, 1] = code, scale[:, 0, :]
        xs[k, 2] = pass3[b]
        for copy in x_copy(k):
            copy.start()

    @pl.loop(0, GROUP)
    def _(k):
        p1(x * GROUP + k)

    same = seg_col == seg_row
    gram = jnp.where(same & (r_id >= c_id), mm(queries, keys, 1, 1), 0.0)
    gh[...], gl[...] = split(gram)
    gram_t = jnp.where(same & (r_id <= c_id), mm(keys, queries, 1, 1), 0.0)
    gth[...], gtl[...] = split(gram_t)
    macc[...] = jnp.zeros_like(macc)
    gacc[...] = jnp.zeros_like(gacc)

    def p2(b):
        bb = (bh[b], bl[b])
        aa = (ah[b], al[b])
        b0 = (bb[0][:, :half], bb[1][:, :half])
        a0 = (aa[0][:, :half], aa[1][:, :half])
        a1 = (aa[0][:, half:], aa[1][:, half:])
        ys[b, :, :half] = mm3(b0, (gth[:half, :half], gtl[:half, :half]))
        ys[b, :, half:] = mm3(bb, (gth[:, half:], gtl[:, half:]))
        zs[b, :, half:] = mm3(a1, (gh[half:, half:], gl[half:, half:]))
        zs[b, :, :half] = mm3(aa, (gh[:, :half], gl[:, :half]))
        macc[:half, :half] += mm3(a0, b0, 0, 0)
        macc[half:, :] += mm3(a1, bb, 0, 0)

    def z_copy(k):
        return (
            (
                rcopy(zq.at[0, k], zqr.at[0, k], zsem, (0, 0, k), me + 2),
                rcopy(zc.at[0, k], zcr.at[0, k], zsem, (0, 1, k), me + 2),
            ),
            (
                rcopy(zq.at[1, k], zqr.at[1, k], zsem, (1, 0, k), me - 2),
                rcopy(zc.at[1, k], zcr.at[1, k], zsem, (1, 1, k), me - 2),
            ),
        )

    def t_copy(k):
        return (
            rcopy(tq.at[k], tqr.at[k], tsem, (0, k), partner),
            rcopy(ts.at[k], tsr.at[k], tsem, (1, k), partner),
        )

    def z_send(way, k, value, copies):
        code, scale = quant(value, 1)
        zq[way, k], zc[way, k] = code, scale[:, 0, :]
        for copy in copies:
            copy.start()

    def z_take(way, k, into, copies):
        for copy in copies:
            copy.wait_recv()
        into[k] = wide(zqr[way, k], zcr[way, k][:, None, :])

    left = x == 0

    def terms(k):
        b = x * GROUP + k
        own, other = pass3[b][:, None, :], xsr[k, 2][:, None, :]
        s_in = wide(xqr[k, 0], xsr[k, 0][:, None, :])
        d_in = wide(xqr[k, 1], xsr[k, 1][:, None, :])
        pass0, pass1 = jnp.where(left, own, other), jnp.where(left, other, own)
        s0, s1 = jnp.where(left, sl[b], s_in), jnp.where(left, s_in, sl[b])
        d0, d1 = jnp.where(left, dlo[b], d_in), jnp.where(left, d_in, dlo[b])
        return pass0, pass1, s0, s1, d0, d1

    @pl.loop(0, GROUP)
    def _(k):
        p2(2 * k)
        for copy in x_copy(k):
            copy.wait_recv()
        pass0, pass1, s0, s1, d0, d1 = terms(k)
        to_next, to_prev = z_copy(k)

        @pl.when(first)
        def _():
            zsr[k] = jnp.zeros_like(s0)

        @pl.when(first & (nz > 1))
        def _():
            z_send(0, k, pass1 * s0 + s1, to_next)

        @pl.when(last)
        def _():
            zdr[k] = jnp.zeros_like(d0)

        @pl.when(last & (nz > 1))
        def _():
            z_send(1, k, d0 + pass0 * d1, to_prev)

        p2(2 * k + 1)

    inner = (z > 0) & (z < nz - 1)
    low = z < nz // 2

    def forward():
        @pl.when(z > 0)
        def _():
            @pl.loop(0, GROUP)
            def _(k):
                to_next = z_copy(k)[0]
                z_take(0, k, zsr, to_next)

                @pl.when(inner)
                def _():
                    pass0, pass1, s0, s1, _, _ = terms(k)
                    z_send(0, k, pass0 * pass1 * zsr[k] + pass1 * s0 + s1, to_next)

    def backward():
        @pl.when(z < nz - 1)
        def _():
            @pl.loop(0, GROUP)
            def _(k):
                to_prev = z_copy(k)[1]
                z_take(1, k, zdr, to_prev)

                @pl.when(inner)
                def _():
                    pass0, pass1, _, _, d0, d1 = terms(k)
                    z_send(1, k, pass0 * pass1 * zdr[k] + d0 + pass0 * d1, to_prev)

    @pl.when(low)
    def _():
        forward()

    backward()

    @pl.when(jnp.logical_not(low))
    def _():
        forward()

    @pl.loop(0, GROUP)
    def _(k):
        b = x * GROUP + k
        pass0, pass1, s0, _, _, d1 = terms(k)
        in0 = zsr[k]
        in1 = pass0 * in0 + s0
        gin1 = zdr[k]
        gin0 = pass1 * gin1 + d1
        code, scale = quant(jnp.where(left, in1, in0), 1)
        tq[k, 0], ts[k, 0] = code, scale[:, 0, :]
        code, scale = quant(jnp.where(left, gin1, gin0), 1)
        tq[k, 1], ts[k, 1] = code, scale[:, 0, :]
        for copy in t_copy(k):
            copy.start()
        ins[b] = jnp.where(left, in0, in1)
        ind[b] = jnp.where(left, gin0, gin1)

    mixed = split(jnp.where(same & (r_id >= c_id), macc[...], 0.0))
    gq_local = mm(mixed[0], keys) + mm(mixed[1], keys)
    gk_local = mm(mixed[0], queries, 0, 0) + mm(mixed[1], queries, 0, 0)

    def p3(b):
        s = split((ins[b] * sd3[b][:, None, :]).reshape(rows, state))
        d = split((ind[b] * ss3[b][:, None, :]).reshape(rows, state))
        qq, kk = qm[...], km[...]
        y = ys[b] + mm(s[0], qq, 1, 1) + mm(s[1], qq, 1, 1)
        zz = zs[b] + mm(d[0], kk, 1, 1) + mm(d[1], kk, 1, 1)
        skip = sk3[b][:, 0:1][:, :, None]
        shape = (hb, width, tok)
        out_ref[hblock(b)] = (
            y.reshape(shape) * e3[b][:, None, :] + skip * sig[hblock(b)].astype(F32)
        ).astype(BF16)
        gs_ref[hblock(b)] = (
            zz.reshape(shape) * f3[b][:, None, :] + skip * cot[hblock(b)].astype(F32)
        ).astype(BF16)
        gacc[:, :state] += mm3((bh[b], bl[b]), d, 0, 0)
        gacc[:, state:] += mm3((ah[b], al[b]), s, 0, 0)

    @pl.loop(0, GROUP)
    def _(k):
        p3(x * GROUP + k)

    @pl.loop(0, GROUP)
    def _(k):
        for copy in t_copy(k):
            copy.wait_recv()
        b = (1 - x) * GROUP + k
        ins[b] = wide(tqr[k, 0], tsr[k, 0][:, None, :])
        ind[b] = wide(tqr[k, 1], tsr[k, 1][:, None, :])
        p3(b)

    piece = tok // nhead
    gk = gk_local + jnp.where(seg_col == seg_last, gacc[:, :state], 0.0)
    gq = gq_local + jnp.where(seg_col == prior, gacc[:, state:], 0.0)
    for j in range(nhead):
        part = slice(j * piece, (j + 1) * piece)
        gg[j, :, :state] = gk[part]
        gg[j, :, state:] = gq[part]

    def h_copy(d):
        to = lax.rem(hd + d, nhead)
        return (
            rcopy(hq.at[to], hqr.at[d], hsem, (0, d), me, to),
            rcopy(hs.at[to], hsr.at[d], hsem, (1, d), me, to),
        )

    def a_copy(d, sender):
        to = lax.rem(hd + d, nhead)
        return rcopy(agb.at[sender], agb.at[sender], asem, (d,), me, to)

    for d in range(1, nhead):
        to = lax.rem(hd + d, nhead)
        code, scale = quant(gg[to], 0)
        hq[to], hs[to] = code, jnp.broadcast_to(scale, hs.shape[1:])
        for copy in h_copy(d):
            copy.start()
    total = gg[hd]
    for d in range(1, nhead):
        for copy in h_copy(d):
            copy.wait_recv()
        total = total + wide(hqr[d], hsr[d][0:1, :])
    agb[hd] = total.astype(BF16)
    for d in range(1, nhead):
        a_copy(d, hd).start()
    for d in range(1, nhead):
        a_copy(d, lax.rem(hd + nhead - d, nhead)).wait_recv()
    for j in range(nhead):
        part = slice(j * piece, (j + 1) * piece)
        gk_ref[part, :] = agb[j, :, :state]
        gq_ref[part, :] = agb[j, :, state:]

    for d in range(1, nhead):
        for copy in h_copy(d):
            copy.wait_send()
        a_copy(d, hd).wait_send()

    @pl.loop(0, GROUP)
    def _(k):
        for copy in x_copy(k) + t_copy(k):
            copy.wait_send()
        to_next, to_prev = z_copy(k)

        @pl.when(z < nz - 1)
        def _():
            for copy in to_next:
                copy.wait_send()

        @pl.when(z > 0)
        def _():
            for copy in to_prev:
                copy.wait_send()


def solution(mesh):
    nseq, nhead = mesh.shape["seq"], mesh.shape["head"]

    def on_device(signal, step_raw, key_proj, query_proj, decay_log, skip_gain, lengths, cotangent):
        tok, heads, width = signal.shape
        state = key_proj.shape[1]
        blocks = 2 * GROUP
        hb = heads // blocks
        rows = hb * width
        piece = tok // nhead
        dma = pltpu.SemaphoreType.DMA
        vmem = pltpu.VMEM
        st = (hb, width, state)
        scratch = (
            [vmem((blocks, rows, tok), BF16)] * 4
            + [vmem((blocks, rows, tok), F32)] * 2
            + [vmem((tok, tok), F32)]
            + [vmem((tok, tok), BF16)] * 4
            + [vmem((tok, state), BF16)] * 2
            + [vmem((blocks, hb, tok), F32)] * 2
            + [vmem((blocks, hb, state), F32)] * 4
            + [vmem((blocks,) + st, F32)] * 2
            + [vmem((GROUP,) + st, F32)] * 2
            + [vmem((blocks,) + st, F32)] * 2
            + [vmem((GROUP, 2) + st, jnp.int16)] * 4
            + [vmem((GROUP, 3, hb, state), F32)] * 2
            + [vmem((2, GROUP) + st, jnp.int16)] * 2
            + [vmem((2, GROUP, hb, state), F32)] * 2
            + [vmem((GROUP, 2, hb, state), F32)] * 2
            + [vmem((nhead, piece, 2 * state), F32)]
            + [vmem((nhead, piece, 2 * state), jnp.int16)] * 2
            + [vmem((nhead, 8, 2 * state), F32)] * 2
            + [vmem((nhead, piece, 2 * state), BF16)]
            + [vmem((tok, 2 * state), F32)]
            + [dma((2, 2, GROUP)), dma((2, 2, 2, GROUP)), dma((2, 2, GROUP))]
            + [dma((2, 2, nhead)), dma((2, nhead))]
        )
        turned = jax.ShapeDtypeStruct((heads, width, tok), BF16)
        grads = jax.ShapeDtypeStruct((tok, state), BF16)
        whole = pl.BlockSpec(memory_space=pltpu.VMEM)
        out, gs, gk, gq = pl.pallas_call(
            functools.partial(kernel, nseq, nhead),
            out_shape=(turned, turned, grads, grads),
            in_specs=[pl.BlockSpec(memory_space=pltpu.SMEM)] + [whole] * 7,
            out_specs=(whole,) * 4,
            scratch_shapes=scratch,
            compiler_params=pltpu.CompilerParams(
                collective_id=0, has_side_effects=True, vmem_limit_bytes=60 << 20
            ),
        )(
            lengths,
            jnp.transpose(signal, (1, 2, 0)),
            jnp.transpose(cotangent, (1, 2, 0)),
            step_raw.T,
            key_proj,
            query_proj,
            decay_log[None, :],
            skip_gain[None, :],
        )
        return jnp.transpose(out, (2, 0, 1)), jnp.transpose(gs, (2, 0, 1)), gk, gq

    in_specs = (
        P("seq", "head", None),
        P("seq", "head"),
        P("seq", None),
        P("seq", None),
        P("head"),
        P("head"),
        P(),
        P("seq", "head", None),
    )
    out_specs = (P("seq", "head", None), P("seq", "head", None), P("seq", None), P("seq", None))
    return jax.shard_map(
        on_device, mesh=mesh, in_specs=in_specs, out_specs=out_specs, check_vma=False
    )
```
